32 devices in a mesh: section: 2 (over x), expert: 16 (over z, y, core).
Axes of the slice: x: 2, y: 2, z: 4, core: 2. Of those that a mesh axis runs over, the one named last changes fastest.
Arguments:
- section_inputs: bfloat16 [2, 1024, 2560], P('section', 'expert'), may hold values from -6 to 6
- incoming: bfloat16 [1, 1024, 2560], P(None, 'expert'), may hold values from -6 to 6
- norm_gain: float32 [2, 2560], P('section'), may hold values from 0.5 to 1.5
- in_weights: bfloat16 [2, 10240, 1536], P('section', 'expert'), may hold values from -0.125 to 0.125
- down_weights: bfloat16 [2, 10240, 768], P('section', 'expert'), may hold values from -0.21875 to 0.21875
- expert_ids: int32 [2, 2, 1024, 2], P(None, 'section', 'expert'), may hold values from 0 to 3, all different within a row; in each aligned block of 64 rows (0 to 63, 64 to 127, ..., all dimensions but the last counted through in order) at most 40 rows name the same one
- route_weights: float32 [2, 2, 1024, 2], P(None, 'section', 'expert'), may hold values from 0.2 to 1
Outputs:
- final_state: bfloat16 [2, 1024, 2560], P('section', 'expert')
The draws below stay inside these ranges and needn't reach their ends.
Inputs may be any that keep to these rules, and one draw needn't show every extreme that they name: `expert_ids`: in each aligned block of 64 tokens (the tokens of one index of expert) of one step and section, no expert is named by more than 40 tokens; a token names 2 different experts.
All inputs are finite; a program needn't handle non-finite values.
Results may differ from the reference program's by a relative error of at most 0.019.
Values may be sent and summed in bfloat16 or wider, within the bound.
No kernel may reach another device: no remote copies, remote signals or barrier semaphores. Data moves between devices by JAX's collectives and lax.ppermute only.
A program may use at most 64 MiB of HBM per device.

```python
import math
import jax
import jax.numpy as jnp
import numpy as np
from jax import lax

D = 2560
FF = 768
GROUP = 4
TOPK = 2
TICKS = 2
TOK_DEV = 64
EXPERTS = 4
CAP = 40
TOKENS = 1024
N_SECTION = 2


def block_levels(rng, dims, cuts, least, high):
    def one(dim, shards_of):
        steps = jax.random.uniform(jax.random.fold_in(jax.random.fold_in(rng, 6), dim), (shards_of,), jnp.float32, least / len(cuts), high / len(cuts))
        return jnp.repeat(jnp.exp(steps), dims[dim] // shards_of).reshape((-1,) + (1,) * (len(dims) - dim - 1))

    factor_of = one(*cuts[0])
    for cut in cuts[1:]:
        factor_of = factor_of * one(*cut)
    return factor_of


def routed_block(stream_key, own, number, rows, number_of, top, most, skew):
    order = jax.random.permutation(stream_key, number_of)
    crowded, common = load_shares(number_of, rows * top, most, skew, True), load_shares(number_of, rows * top, most, skew, False)
    places = jnp.arange(number_of)

    def named(sizes, turn):
        used = int((sizes > 0).sum())
        fixed = max(1, used // 4)
        passed = fixed + (places - fixed + turn * (used - fixed)) % max(1, number_of - fixed)
        return jnp.zeros((number_of,), jnp.int32).at[order[jnp.where(places < fixed, places, passed)]].set(jnp.asarray(sizes, jnp.int32))

    sizes = jnp.where(number % 4 == 0, named(crowded, number // 4), named(common, number - number // 4 - 1))
    mixed = jax.random.permutation(jax.random.fold_in(own, 3), number_of)
    source_of, taker = mixed[0:number_of // 2 * 2:2], mixed[1:number_of // 2 * 2:2]
    room = jnp.minimum(sizes[source_of] - 1, most - sizes[taker]) // 2
    room = jnp.where((source_of == order[0]) | (taker == order[0]) | (sizes[taker] == 0), 0, jnp.maximum(room, 0))
    passed = jax.random.randint(jax.random.fold_in(own, 4), (number_of // 2,), 0, 1 << 20) % (room + 1)
    sizes = sizes.at[source_of].add(-passed).at[taker].add(passed)
    labels = jnp.searchsorted(jnp.cumsum(sizes), jnp.arange(rows * top), side="right").astype(jnp.int32)
    table = labels.reshape(top, rows).T
    table = table[jax.random.permutation(jax.random.fold_in(own, 1), rows)]
    turn = jax.random.randint(jax.random.fold_in(own, 2), (rows, 1), 0, top)
    return jnp.take_along_axis(table, (jnp.arange(top)[None, :] + turn) % top, axis=1)


def load_shares(count, total, reach, lean, full):
    loads = [(1 << 20) // math.isqrt(rank ** lean) + 1 for rank in range(1, count + 1)]
    largest = reach if full else min(reach, max(-(-total // count), total * loads[0] // sum(loads)))
    least = 1 if total - largest >= count - 1 else 0
    counts, rest = [largest] + [least] * (count - 1), total - largest - least * (count - 1)
    while rest > 0:
        free = [i for i in range(1, count) if counts[i] < largest] or [i for i in range(1, count) if counts[i] < reach]
        whole, left = sum([loads[i] for i in free]), rest
        for i in free:
            extra = min(reach - counts[i], max(1, left * loads[i] // whole), rest)
            counts[i] = counts[i] + extra
            rest = rest - extra
    return np.array(counts)


def centred(key, extent, spread, bound, pieces=(), kind=jnp.bfloat16):
    loudness = block_levels(key, extent, pieces, -0.22, 0.18) if pieces else 1.0
    array = jax.random.normal(key, extent, jnp.float32) * spread * loudness
    return jnp.minimum(jnp.maximum(array, -bound), bound).astype(kind)


def setup_inputs(seed: int = 0) -> dict:
    streams_of = jax.random.split(jax.random.key(seed), 8)
    section_inputs = centred(streams_of[0], (N_SECTION, TOKENS, D), 1.0, 6.0, ((0, 2), (1, 16)))
    incoming = centred(streams_of[1], (TICKS - 1, TOKENS, D), 1.0, 6.0, ((1, 16),))
    norm_gain = jnp.clip(1.0 + 0.1 * jax.random.normal(streams_of[2], (N_SECTION, D), jnp.float32), 0.5, 1.5)
    in_weights = centred(streams_of[3], (N_SECTION, EXPERTS * D, 2 * FF), D ** -0.5, 0.125, ((0, 2), (1, 16)))
    down_weights = centred(streams_of[4], (N_SECTION, EXPERTS * D, FF), FF ** -0.5, 0.21875, ((0, 2), (1, 16)))
    expert_ids_keys = jax.random.split(jax.random.fold_in(streams_of[5], 1), TICKS * N_SECTION * TOKENS // TOK_DEV)
    expert_ids_turns = jax.random.permutation(jax.random.fold_in(streams_of[5], 3), TICKS * N_SECTION * TOKENS // TOK_DEV)
    expert_ids = jax.vmap(lambda own, number: routed_block(jax.random.fold_in(streams_of[5], 2), own, number, TOK_DEV, EXPERTS, TOPK, CAP, 2))(expert_ids_keys, expert_ids_turns).reshape((TICKS, N_SECTION, TOKENS, TOPK))
    route_weights = jnp.clip(0.2 + 0.8 * jax.random.uniform(streams_of[6], (TICKS, N_SECTION, TOKENS, TOPK), jnp.float32) ** block_levels(streams_of[6], (TICKS, N_SECTION, TOKENS, TOPK), ((1, 2), (2, 16)), -0.2, 0.2), 0.2, 1.0)
    return {"section_inputs": section_inputs, "incoming": incoming, "norm_gain": norm_gain, "in_weights": in_weights, "down_weights": down_weights, "expert_ids": expert_ids, "route_weights": route_weights}


def norm_rows(inputs, scale_row):
    widened = inputs.astype(jnp.float32)
    mean_square = lax.optimization_barrier(jnp.mean(widened * widened, axis=-1, keepdims=True))
    return (widened * lax.rsqrt(mean_square + 1e-06) * scale_row).astype(jnp.bfloat16)

def slot_tables(block_ids, block_weights):
    flat_ids = block_ids.reshape(-1)
    flat_weights = block_weights.reshape(-1)
    onehot = (flat_ids[:, None] == jnp.arange(EXPERTS, dtype=jnp.int32)[None, :]).astype(jnp.int32)
    before = jnp.cumsum(onehot, axis=0) - onehot
    slot_index = lax.optimization_barrier(jnp.sum(before * onehot, axis=1))
    slot_hot = (slot_index[:, None] == jnp.arange(CAP, dtype=jnp.int32)[None, :]).astype(jnp.float32)
    token_of = jnp.arange(TOK_DEV * TOPK, dtype=jnp.int32) // TOPK
    owner = (token_of[:, None] == jnp.arange(TOK_DEV, dtype=jnp.int32)[None, :]).astype(jnp.float32)
    expert_hot = onehot.astype(jnp.float32)
    picker = jnp.einsum('ae,ac,at->ect', expert_hot, slot_hot, owner)
    blender = jnp.einsum('ae,ac,at,a->tec', expert_hot, slot_hot, owner, flat_weights)
    return (picker, blender)

def expert_apply(token_rows, in_weight, down_weight, group_size):
    row_total = token_rows.shape[0]
    slice_width = D // group_size
    partials = jnp.einsum('rgd,gdh->grh', token_rows.reshape(row_total, group_size, slice_width).astype(jnp.float32), in_weight.reshape(group_size, slice_width, 2 * FF).astype(jnp.float32))
    rounded = lax.optimization_barrier(partials.astype(jnp.bfloat16))
    summed = lax.optimization_barrier(jnp.sum(rounded.astype(jnp.float32), axis=0))
    active = (jax.nn.silu(summed[:, :FF]) * summed[:, FF:]).astype(jnp.bfloat16)
    produced = lax.dot_general(active, down_weight, (((1,), (1,)), ((), ())), preferred_element_type=jnp.float32)
    return produced.astype(jnp.bfloat16)

def layer(inputs, scale_row, in_weights, down_weights, ids_now, weights_now):
    normed = norm_rows(inputs, scale_row)
    blocks = TOKENS // TOK_DEV
    picker, blender = jax.vmap(slot_tables)(ids_now.reshape(blocks, TOK_DEV, TOPK), weights_now.reshape(blocks, TOK_DEV, TOPK))
    dispatched = jnp.einsum('bect,btd->ebcd', picker, normed.reshape(blocks, TOK_DEV, D).astype(jnp.float32)).astype(jnp.bfloat16)

    def one_expert(operands):
        expert_rows, in_weight, down_weight = operands
        return expert_apply(expert_rows.reshape(blocks * CAP, D), in_weight, down_weight, GROUP)
    expert_outputs = lax.map(one_expert, (dispatched, in_weights.reshape(EXPERTS, D, 2 * FF), down_weights.reshape(EXPERTS, D, FF)))
    expert_outputs = expert_outputs.reshape(EXPERTS, blocks, CAP, D)
    mixture = jnp.einsum('btec,ebcd->btd', blender, expert_outputs.astype(jnp.float32))
    return (inputs.astype(jnp.float32) + mixture.reshape(TOKENS, D)).astype(jnp.bfloat16)

def reference(section_inputs, incoming, norm_gain, in_weights, down_weights, expert_ids, route_weights):

    def apply_section(operands):
        return layer(*operands)
    current = section_inputs
    for step_index in range(TICKS):
        current = lax.map(apply_section, (current, norm_gain, in_weights, down_weights, expert_ids[step_index], route_weights[step_index]))
        if step_index + 1 < TICKS:
            current = jnp.concatenate([incoming[step_index][None], current[:-1]], axis=0)
    return current
```

```python
import functools

import jax
import jax.numpy as jnp
from jax import lax
from jax.experimental import pallas as pl
from jax.experimental.pallas import tpu as pltpu
from jax.sharding import PartitionSpec as P

GROUP = 4
TOPK = 2
TICKS = 2
CHUNKS = 2


def swapped(block, flip):
    return lax.ppermute(block, "expert", [(i, i ^ flip) for i in range(lax.axis_size("expert"))])


def onward(block, flip, ahead=1):
    sections, span = lax.axis_size("section"), lax.axis_size("expert")
    route = []
    for s in range(sections):
        for i in range(span):
            route.append((s * span + i, (s + ahead) % sections * span + (i ^ flip)))
    return lax.ppermute(block, ("section", "expert"), route)


def call(kernel, outs, *operands, scalars=0):
    specs = [pl.BlockSpec(memory_space=pltpu.SMEM)] * scalars
    specs += [pl.BlockSpec(memory_space=pltpu.VMEM)] * (len(operands) - scalars)
    return pl.pallas_call(
        kernel,
        out_shape=outs,
        in_specs=specs,
        out_specs=[pl.BlockSpec(memory_space=pltpu.VMEM)] * len(outs),
        compiler_params=pltpu.CompilerParams(vmem_limit_bytes=24 << 20),
    )(*operands)


def dot(a, b, contract):
    return lax.dot_general(a, b, (contract, ((), ())), preferred_element_type=jnp.float32)


def pick_kernel(picker, source, *outs):
    rows = outs[0].shape[0]
    for k, out in enumerate(outs):
        taken = dot(picker[k * rows : (k + 1) * rows, :], source[...], ((1,), (0,)))
        out[...] = taken.astype(out.dtype)


def in_kernel(count, *refs):
    mine, theirs = refs[:count], refs[count : 2 * count]
    weight_mine, weight_theirs, out = refs[2 * count :]
    width = weight_mine.shape[1]
    rows = mine[0].shape[0]
    for k in range(count):
        a, b = mine[k][...], theirs[k][...]
        part = dot(a, weight_mine[...], ((1,), (0,))) + dot(b, weight_theirs[...], ((1,), (0,)))
        at = pl.ds(k * rows, rows)
        out[at, 0:width] = part.astype(out.dtype)
        a, b = a.astype(jnp.float32), b.astype(jnp.float32)
        square = jnp.sum(a * a + b * b, axis=1, keepdims=True)
        high = square.astype(out.dtype).astype(jnp.float32)
        lane = lax.broadcasted_iota(jnp.int32, (rows, 128), 1)
        pair = jnp.where(lane < 64, high, square - high)
        out[at, width : width + 128] = pair.astype(out.dtype)


def act_kernel(features, mine, theirs, out):
    half = out.shape[1]
    tail_a = mine[:, 2 * half :].astype(jnp.float32)
    tail_b = theirs[:, 2 * half :].astype(jnp.float32)
    tail = tail_a + tail_b
    square = tail[:, 0:1] + tail[:, 64:65]
    inverse = lax.rsqrt(square * (1.0 / features) + 1e-06)
    gate = mine[:, :half].astype(jnp.float32) + theirs[:, :half].astype(jnp.float32)
    up = mine[:, half : 2 * half].astype(jnp.float32) + theirs[:, half : 2 * half].astype(jnp.float32)
    gate = gate * inverse
    up = up * inverse
    out[...] = (gate / (1.0 + jnp.exp(-gate)) * up).astype(out.dtype)


def out_kernel(core, mine, theirs, weight, *outs):
    half = mine.shape[1]
    rows = outs[0].shape[0]
    first = core[0] == 0
    for k, out in enumerate(outs):
        a, b = mine[k * rows : (k + 1) * rows, :], theirs[k * rows : (k + 1) * rows, :]
        low, high = jnp.where(first, a, b), jnp.where(first, b, a)
        made = dot(low, weight[:, :half], ((1,), (1,))) + dot(high, weight[:, half:], ((1,), (1,)))
        out[...] = made.astype(out.dtype)


def blend(blender, returned):
    rows = returned[0].shape[0]
    total = None
    for k, block in enumerate(returned):
        part = dot(blender[k * rows : (k + 1) * rows, :], block[...], ((0,), (0,)))
        total = part if total is None else total + part
    return total


def relay_kernel(count, last, *refs):
    blender, current, entering, picker = refs[:4]
    returned, carried, outs = refs[4 : 4 + count], refs[4 + count], refs[5 + count :]
    fresh = (current[...].astype(jnp.float32) + blend(blender, returned)).astype(carried.dtype)
    carried[...] = fresh
    source = jnp.where(last[0] == 1, entering[...], fresh)
    rows = outs[0].shape[0]
    for k, out in enumerate(outs):
        taken = dot(picker[k * rows : (k + 1) * rows, :], source, ((1,), (0,)))
        out[...] = taken.astype(out.dtype)


def final_kernel(count, first, *refs):
    blender, handed, entering = refs[:3]
    returned, out = refs[3 : 3 + count], refs[3 + count]
    before = jnp.where(first[0] == 1, entering[...], handed[...]).astype(jnp.float32)
    out[...] = (before + blend(blender, returned)).astype(out.dtype)


def body(section_inputs, incoming, norm_gain, in_weights, down_weights, expert_ids, route_weights):
    span = lax.axis_size("expert")
    sections = lax.axis_size("section")
    experts = span // GROUP
    tokens, features = section_inputs.shape[1:]
    width, hidden = in_weights.shape[1], down_weights.shape[2]
    half = hidden // 2
    capacity = min(tokens, max(2, TOPK * tokens * 5 // (4 * experts)))
    blocks = GROUP // CHUNKS
    rows = -(-blocks * capacity // 16) * 16
    together = blocks * tokens
    position = lax.axis_index("expert")
    member, place = position % GROUP, position // GROUP
    core, chip = member & 1, member >> 1 & 1
    section = lax.axis_index("section")
    first = (section == 0).astype(jnp.int32).reshape(1)
    last = (section == sections - 1).astype(jnp.int32).reshape(1)
    core_flag = core.reshape(1)
    narrow = section_inputs.dtype

    def ordered(parts, axis):
        low = [jnp.where(core == 0, parts[i], parts[i + 1]) for i in (0, 2)]
        high = [jnp.where(core == 0, parts[i + 1], parts[i]) for i in (0, 2)]
        pairs = [jnp.concatenate([a, b], axis) for a, b in zip(low, high)]
        return [jnp.where(chip == 0, pairs[0], pairs[1]), jnp.where(chip == 0, pairs[1], pairs[0])]

    def to_slices(block):
        parts = []
        for j in range(GROUP):
            piece = lax.dynamic_slice_in_dim(block, (member ^ j) * width, width, 1)
            parts.append(swapped(piece, j) if j else piece)
        return ordered(parts, 0)

    def to_rows(chunks):
        same = jnp.where(chip == 0, chunks[0], chunks[1])
        other = jnp.where(chip == 0, chunks[1], chunks[0])
        parts = []
        for j, pair in enumerate((same, same, other, other)):
            lower = (core ^ (j & 1)) == 0
            piece = jnp.where(lower, pair[:tokens], pair[tokens:])
            parts.append(swapped(piece, j) if j else piece)
        halves = [jnp.concatenate(cut, 1) for cut in (
            (jnp.where(core == 0, parts[0], parts[1]), jnp.where(core == 0, parts[1], parts[0])),
            (jnp.where(core == 0, parts[2], parts[3]), jnp.where(core == 0, parts[3], parts[2])),
        )]
        pair = (jnp.where(chip == 0, halves[0], halves[1]), jnp.where(chip == 0, halves[1], halves[0]))
        return jnp.concatenate(pair, 1)

    start = to_slices(section_inputs[0])

    facts = jnp.concatenate([expert_ids[:, 0].astype(jnp.float32), route_weights[:, 0]], -1)
    facts = jnp.transpose(facts, (0, 2, 1)).reshape(2 * TICKS * TOPK, tokens)
    facts = ordered([facts] + [swapped(facts, j) for j in range(1, GROUP)], 1)
    facts = jnp.concatenate(facts, 1)
    ahead = onward(facts, 0, sections - 1)

    index = jnp.arange(GROUP * tokens, dtype=jnp.int32)
    earlier = (index[:, None] < index[None, :]) & (index[:, None] // tokens == index[None, :] // tokens)
    earlier = earlier.astype(narrow)
    names = (place ^ jnp.arange(experts, dtype=jnp.int32)).astype(jnp.float32)[:, None]

    def tables(table, step, weighted):
        base = 2 * TOPK * step
        hits = [(table[base + r][None, :] == names) for r in range(TOPK)]
        hit = functools.reduce(jnp.logical_or, hits)
        slot = dot(hit.astype(narrow), earlier, ((1,), (0,)))
        slot = slot.astype(jnp.int32) + (index // tokens % blocks * capacity)[None, :]
        slot = jnp.where(hit, slot, -1)
        made = []
        for t in range(CHUNKS):
            cut = slice(t * together, (t + 1) * together)
            line = jnp.arange(rows, dtype=jnp.int32)[None, :, None]
            match = slot[:, None, cut] == line
            picker = match.astype(narrow).reshape(experts * rows, together)
            blender = None
            if weighted:
                weight = sum(
                    jnp.where(hits[r], table[base + TOPK + r][None, :], 0.0) for r in range(TOPK)
                )
                blender = jnp.where(match, weight[:, None, cut], 0.0).astype(narrow)
                blender = blender.reshape(experts * rows, together)
            made.append((picker, blender))
        return made

    now = tables(facts, 0, True)
    later = tables(facts, 1, True)
    onto = tables(ahead, 1, False)

    gain = lax.dynamic_slice_in_dim(norm_gain[0], member * width, width)
    scaled = (in_weights[0].astype(jnp.float32) * gain[:, None]).astype(narrow)

    def half_of(which):
        cuts = [lax.dynamic_slice_in_dim(scaled, s * hidden + which * half, half, 1) for s in range(2)]
        return jnp.concatenate(cuts, 1)

    weight_mine = half_of(core)
    weight_theirs = swapped(half_of(1 - core), 1)
    down = down_weights[0]
    entering = to_slices(incoming[0])

    row_block = jax.ShapeDtypeStruct((rows, width), narrow)
    chunk_block = jax.ShapeDtypeStruct((together, width), narrow)

    def experts_on(arrived):
        theirs = [swapped(block, 1) for block in arrived]
        (partial,) = call(
            functools.partial(in_kernel, experts),
            [jax.ShapeDtypeStruct((experts * rows, hidden + 128), narrow)],
            *arrived, *theirs, weight_mine, weight_theirs,
        )
        (active,) = call(
            functools.partial(act_kernel, float(features)),
            [jax.ShapeDtypeStruct((experts * rows, half), narrow)],
            partial, swapped(partial, 2),
        )
        made = call(
            out_kernel, [row_block] * experts, core_flag, active, swapped(active, 1), down, scalars=1
        )
        return [made[0]] + [swapped(made[k], k * GROUP) for k in range(1, experts)]

    finals = []
    for t in range(CHUNKS):
        picked = call(pick_kernel, [row_block] * experts, now[t][0], start[t])
        arrived = [picked[0]] + [swapped(picked[k], k * GROUP) for k in range(1, experts)]
        returned = experts_on(arrived)
        carried, *picked = call(
            functools.partial(relay_kernel, experts), [chunk_block] + [row_block] * experts,
            last, now[t][1], start[t], entering[t], onto[t][0], *returned, scalars=1,
        )
        arrived = [onward(block, k * GROUP) for k, block in enumerate(picked)]
        handed = onward(carried, 0)
        returned = experts_on(arrived)
        (final,) = call(
            functools.partial(final_kernel, experts), [chunk_block],
            first, later[t][1], handed, entering[t], *returned, scalars=1,
        )
        finals.append(final)
    return to_rows(finals)[None]


def solution(mesh):
    placed = (
        P("section", "expert", None),
        P(None, "expert", None),
        P("section", None),
        P("section", "expert", None),
        P("section", "expert", None),
        P(None, "section", "expert", None),
        P(None, "section", "expert", None),
    )
    return jax.shard_map(
        body, mesh=mesh, in_specs=placed, out_specs=P("section", "expert", None), check_vma=False
    )
```

```python
import functools

import jax
import jax.numpy as jnp
from jax import lax
from jax.experimental import pallas as pl
from jax.experimental.pallas import tpu as pltpu
from jax.sharding import PartitionSpec as P

GROUP = 4
TOPK = 2
TICKS = 2
CHUNKS = 2


def swapped(block, flip):
    return lax.ppermute(block, "expert", [(i, i ^ flip) for i in range(lax.axis_size("expert"))])


def onward(block, flip, ahead=1):
    sections, span = lax.axis_size("section"), lax.axis_size("expert")
    route = []
    for s in range(sections):
        for i in range(span):
            route.append((s * span + i, (s + ahead) % sections * span + (i ^ flip)))
    return lax.ppermute(block, ("section", "expert"), route)


def call(kernel, outs, *operands, scalars=0, after=()):
    count = len(operands)

    def wrapped(*refs):
        kernel(*refs[:count], *refs[count + len(after) :])

    specs = [pl.BlockSpec(memory_space=pltpu.SMEM)] * scalars
    specs += [pl.BlockSpec(memory_space=pltpu.VMEM)] * (count - scalars)
    specs += [pl.BlockSpec(memory_space=pl.ANY)] * len(after)
    return pl.pallas_call(
        wrapped,
        out_shape=outs,
        in_specs=specs,
        out_specs=[pl.BlockSpec(memory_space=pltpu.VMEM)] * len(outs),
        compiler_params=pltpu.CompilerParams(vmem_limit_bytes=24 << 20),
    )(*operands, *after)


def dot(a, b, contract):
    return lax.dot_general(a, b, (contract, ((), ())), preferred_element_type=jnp.float32)


def table_kernel(shape, step, wanted, place, facts, *outs):
    experts, rows, tokens, capacity = shape
    total = facts.shape[1]
    together = total // CHUNKS
    lines = max(16, experts)
    names = (place[0] ^ lax.broadcasted_iota(jnp.int32, (lines, total), 0)).astype(jnp.float32)
    base = 2 * TOPK * step
    hits = [facts[base + r : base + r + 1, :] == names for r in range(TOPK)]
    weight = 0.0
    hit = None
    for r, one in enumerate(hits):
        weight = weight + jnp.where(one, facts[base + TOPK + r : base + TOPK + r + 1, :], 0.0)
        hit = one if hit is None else hit | one
    row = lax.broadcasted_iota(jnp.int32, (total, total), 0)
    column = lax.broadcasted_iota(jnp.int32, (total, total), 1)
    row_block = sum((row >= b * tokens).astype(jnp.int32) for b in range(1, GROUP))
    column_block = sum((column >= b * tokens).astype(jnp.int32) for b in range(1, GROUP))
    earlier = jnp.where((row < column) & (row_block == column_block), 1.0, 0.0)
    slot = dot(jnp.where(hit, 1.0, 0.0).astype(jnp.bfloat16), earlier.astype(jnp.bfloat16), ((1,), (0,)))
    lane = lax.broadcasted_iota(jnp.int32, (lines, total), 1)
    for b in range(1, GROUP):
        step_up = capacity if b % (GROUP // CHUNKS) else -capacity * (GROUP // CHUNKS - 1)
        slot = slot + jnp.where(lane >= b * tokens, float(step_up), 0.0)
    slot = jnp.where(hit, slot, -1.0)
    line = lax.broadcasted_iota(jnp.int32, (rows, together), 0).astype(jnp.float32)
    for t in range(CHUNKS):
        cut = slice(t * together, (t + 1) * together)
        for k in range(experts):
            match = slot[k : k + 1, cut] == line
            at = pl.ds(k * rows, rows)
            made = outs[t * len(wanted) : (t + 1) * len(wanted)]
            for kind, out in zip(wanted, made):
                value = 1.0 if kind == "pick" else weight[k : k + 1, cut]
                out[at, :] = jnp.where(match, value, 0.0).astype(out.dtype)


def take(picker, source, outs):
    rows = outs[0].shape[0]
    for k, out in enumerate(outs):
        taken = dot(picker[k * rows : (k + 1) * rows, :], source, ((1,), (0,)))
        out[...] = taken.astype(out.dtype)


def enter_kernel(experts, core, chip, *refs):
    parts, pickers, outs = refs[:GROUP], refs[GROUP : GROUP + CHUNKS], refs[GROUP + CHUNKS :]
    tokens = parts[0].shape[0]
    even, near = core[0] == 0, chip[0] == 0
    for t in range(CHUNKS):
        mine = near if t == 0 else jnp.logical_not(near)
        for h in range(GROUP // CHUNKS):
            straight = even if h == 0 else jnp.logical_not(even)
            same = jnp.where(straight, parts[0][...], parts[1][...])
            other = jnp.where(straight, parts[2][...], parts[3][...])
            outs[t][h * tokens : (h + 1) * tokens, :] = jnp.where(mine, same, other)
        made = outs[CHUNKS + t * experts : CHUNKS + (t + 1) * experts]
        take(pickers[t], outs[t][...], made)


def prepare_kernel(core, weight, gain, mine, theirs):
    even = core[0] == 0
    half = mine.shape[1] // 2
    for s in range(2):
        low = weight[:, 2 * s * half : (2 * s + 1) * half].astype(jnp.float32) * gain[...]
        high = weight[:, (2 * s + 1) * half : (2 * s + 2) * half].astype(jnp.float32) * gain[...]
        mine[:, s * half : (s + 1) * half] = jnp.where(even, low, high).astype(mine.dtype)
        theirs[:, s * half : (s + 1) * half] = jnp.where(even, high, low).astype(theirs.dtype)


def in_kernel(count, *refs):
    mine, theirs = refs[:count], refs[count : 2 * count]
    weight_mine, weight_theirs, out = refs[2 * count :]
    width = weight_mine.shape[1]
    rows = mine[0].shape[0]
    for k in range(count):
        a, b = mine[k][...], theirs[k][...]
        part = dot(a, weight_mine[...], ((1,), (0,))) + dot(b, weight_theirs[...], ((1,), (0,)))
        at = pl.ds(k * rows, rows)
        out[at, 0:width] = part.astype(out.dtype)
        a, b = a.astype(jnp.float32), b.astype(jnp.float32)
        square = jnp.sum(a * a + b * b, axis=1, keepdims=True)
        high = square.astype(out.dtype).astype(jnp.float32)
        lane = lax.broadcasted_iota(jnp.int32, (rows, 128), 1)
        pair = jnp.where(lane < 64, high, square - high)
        out[at, width : width + 128] = pair.astype(out.dtype)


def act_kernel(features, mine, theirs, out):
    half = out.shape[1]
    tail_a = mine[:, 2 * half :].astype(jnp.float32)
    tail_b = theirs[:, 2 * half :].astype(jnp.float32)
    tail = tail_a + tail_b
    square = tail[:, 0:1] + tail[:, 64:65]
    inverse = lax.rsqrt(square * (1.0 / features) + 1e-06)
    gate = mine[:, :half].astype(jnp.float32) + theirs[:, :half].astype(jnp.float32)
    up = mine[:, half : 2 * half].astype(jnp.float32) + theirs[:, half : 2 * half].astype(jnp.float32)
    gate = gate * inverse
    up = up * inverse
    out[...] = (gate / (1.0 + jnp.exp(-gate)) * up).astype(out.dtype)


def out_kernel(core, mine, theirs, weight, *outs):
    half = mine.shape[1]
    rows = outs[0].shape[0]
    first = core[0] == 0
    for k, out in enumerate(outs):
        a, b = mine[k * rows : (k + 1) * rows, :], theirs[k * rows : (k + 1) * rows, :]
        low, high = jnp.where(first, a, b), jnp.where(first, b, a)
        made = dot(low, weight[:, :half], ((1,), (1,))) + dot(high, weight[:, half:], ((1,), (1,)))
        out[...] = made.astype(out.dtype)


def blend(blender, returned):
    rows = returned[0].shape[0]
    total = None
    for k, block in enumerate(returned):
        part = dot(blender[k * rows : (k + 1) * rows, :], block[...], ((0,), (0,)))
        total = part if total is None else total + part
    return total


def relay_kernel(count, last, *refs):
    blender, current, entering, picker = refs[:4]
    returned, carried, outs = refs[4 : 4 + count], refs[4 + count], refs[5 + count :]
    fresh = (current[...].astype(jnp.float32) + blend(blender, returned)).astype(carried.dtype)
    carried[...] = fresh
    take(picker, jnp.where(last[0] == 1, entering[...], fresh), outs)


def final_kernel(count, first, *refs):
    blender, handed, entering = refs[:3]
    returned, out = refs[3 : 3 + count], refs[3 + count]
    before = jnp.where(first[0] == 1, entering[...], handed[...]).astype(jnp.float32)
    out[...] = (before + blend(blender, returned)).astype(out.dtype)


def body(section_inputs, incoming, norm_gain, in_weights, down_weights, expert_ids, route_weights):
    span = lax.axis_size("expert")
    sections = lax.axis_size("section")
    experts = span // GROUP
    tokens, features = section_inputs.shape[1:]
    width, hidden = in_weights.shape[1], down_weights.shape[2]
    half = hidden // 2
    capacity = min(tokens, max(2, TOPK * tokens * 5 // (4 * experts)))
    blocks = GROUP // CHUNKS
    rows = -(-blocks * capacity // 16) * 16
    together = blocks * tokens
    position = lax.axis_index("expert")
    member, place = position % GROUP, position // GROUP
    core, chip = member & 1, member >> 1 & 1
    section = lax.axis_index("section")
    first = (section == 0).astype(jnp.int32).reshape(1)
    last = (section == sections - 1).astype(jnp.int32).reshape(1)
    core_flag, chip_flag, place_flag = core.reshape(1), chip.reshape(1), place.reshape(1)
    narrow = section_inputs.dtype
    row_block = jax.ShapeDtypeStruct((rows, width), narrow)
    chunk_block = jax.ShapeDtypeStruct((together, width), narrow)
    table_block = jax.ShapeDtypeStruct((experts * rows, together), narrow)

    def ordered(parts, axis):
        low = [jnp.where(core == 0, parts[i], parts[i + 1]) for i in (0, 2)]
        high = [jnp.where(core == 0, parts[i + 1], parts[i]) for i in (0, 2)]
        pairs = [jnp.concatenate([a, b], axis) for a, b in zip(low, high)]
        return [jnp.where(chip == 0, pairs[0], pairs[1]), jnp.where(chip == 0, pairs[1], pairs[0])]

    def to_slices(block):
        parts = []
        for j in range(GROUP):
            piece = lax.dynamic_slice_in_dim(block, (member ^ j) * width, width, 1)
            parts.append(swapped(piece, j) if j else piece)
        return parts

    def to_rows(chunks):
        same = jnp.where(chip == 0, chunks[0], chunks[1])
        other = jnp.where(chip == 0, chunks[1], chunks[0])
        parts = []
        for j, pair in enumerate((same, same, other, other)):
            lower = (core ^ (j & 1)) == 0
            piece = jnp.where(lower, pair[:tokens], pair[tokens:])
            parts.append(swapped(piece, j) if j else piece)
        return jnp.concatenate(ordered(parts, 1), 1)

    facts = jnp.concatenate([expert_ids[:, 0].astype(jnp.float32), route_weights[:, 0]], -1)
    facts = jnp.transpose(facts, (0, 2, 1)).reshape(2 * TICKS * TOPK, tokens)
    facts = ordered([facts] + [swapped(facts, j) for j in range(1, GROUP)], 1)
    facts = jnp.concatenate(facts, 1)

    def tables(table, step, wanted):
        made = call(
            functools.partial(table_kernel, (experts, rows, tokens, capacity), step, wanted),
            [table_block] * (CHUNKS * len(wanted)), place_flag, table, scalars=1,
        )
        return [made[t * len(wanted) : (t + 1) * len(wanted)] for t in range(CHUNKS)]

    now = tables(facts, 0, ("pick", "blend"))
    entered = call(
        functools.partial(enter_kernel, experts), [chunk_block] * CHUNKS + [row_block] * (CHUNKS * experts),
        core_flag, chip_flag, *to_slices(section_inputs[0]), *[now[t][0] for t in range(CHUNKS)], scalars=2,
    )
    start, picked = entered[:CHUNKS], entered[CHUNKS:]
    arrived = []
    for t in range(CHUNKS):
        own = picked[t * experts : (t + 1) * experts]
        arrived.append([own[0]] + [swapped(own[k], k * GROUP) for k in range(1, experts)])

    incoming, facts, gain, _ = lax.optimization_barrier((incoming, facts, norm_gain, start[0]))
    gain = lax.dynamic_slice_in_dim(gain[0], member * width, width)[:, None]
    scaled = jax.ShapeDtypeStruct((width, hidden), narrow)
    weight_mine, weight_theirs = call(
        prepare_kernel, [scaled] * 2, core_flag, in_weights[0], gain, scalars=1, after=(start[0],)
    )
    weight_theirs = swapped(weight_theirs, 1)
    down = down_weights[0]
    entering = ordered(to_slices(incoming[0]), 0)
    onto = tables(onward(facts, 0, sections - 1), 1, ("pick",))
    later = tables(facts, 1, ("blend",))

    def experts_on(arrived, latest):
        partial, returned = [], []
        for t in range(CHUNKS):
            theirs = [swapped(block, 1) for block in arrived[t]]
            latest = call(
                functools.partial(in_kernel, experts),
                [jax.ShapeDtypeStruct((experts * rows, hidden + 128), narrow)],
                *arrived[t], *theirs, weight_mine, weight_theirs, after=(latest,),
            )[0]
            partial.append(latest)
        for t in range(CHUNKS):
            active = call(
                functools.partial(act_kernel, float(features)),
                [jax.ShapeDtypeStruct((experts * rows, half), narrow)],
                partial[t], swapped(partial[t], 2), after=(latest,),
            )[0]
            made = call(
                out_kernel, [row_block] * experts, core_flag, active, swapped(active, 1), down, scalars=1
            )
            latest = made[0]
            returned.append([made[0]] + [swapped(made[k], k * GROUP) for k in range(1, experts)])
        return returned, partial, latest

    returned, _, latest = experts_on(arrived, start[0])
    arrived, carried = [], []
    for t in range(CHUNKS):
        latest, *picked = call(
            functools.partial(relay_kernel, experts), [chunk_block] + [row_block] * experts,
            last, now[t][1], start[t], entering[t], onto[t][0], *returned[t], scalars=1, after=(latest,),
        )
        carried.append(latest)
        arrived.append([onward(block, k * GROUP) for k, block in enumerate(picked)])
    returned, partial, latest = experts_on(arrived, latest)
    carried = lax.optimization_barrier((*carried, partial[-1]))[:CHUNKS]
    finals = []
    for t in range(CHUNKS):
        latest = call(
            functools.partial(final_kernel, experts), [chunk_block],
            first, later[t][0], onward(carried[t], 0), entering[t], *returned[t], scalars=1, after=(latest,),
        )[0]
        finals.append(latest)
    return to_rows(finals)[None]


def solution(mesh):
    placed = (
        P("section", "expert", None),
        P(None, "expert", None),
        P("section", None),
        P("section", "expert", None),
        P("section", "expert", None),
        P(None, "section", "expert", None),
        P(None, "section", "expert", None),
    )
    return jax.shard_map(
        body, mesh=mesh, in_specs=placed, out_specs=P("section", "expert", None), check_vma=False
    )
```
